128 devices in a mesh: mode: 8 (over x_hi, z), tile: 16 (over y, x_lo, core).
Axes of the slice: x: 4 (x_hi: 2, x_lo: 2; x = x_hi * 2 + x_lo), y: 4, z: 4, core: 2. Of those that a mesh axis runs over, the one named last changes fastest.
Arguments:
- distribution: float32 [4096, 128, 128], P('mode', 'tile'), may hold values from -6 to 6
- courant: float32 [2, 4096], P(None, 'mode'), may hold values from -0.4 to 0.4
- relax_rate: float32 [4096], P('mode'), may hold values from 0.1 to 2
- scatter_weight: float32 [4096, 4096], P('mode'), may hold values from -0.09375 to 0.09375
- cell_flags: int32 [128, 128], P('tile'), may hold values 0 or 1
Outputs:
- evolved: float32 [4096, 128, 128], P('mode', 'tile')
The draws below stay inside these ranges and needn't reach their ends.
All inputs are finite; a program needn't handle non-finite values. No bound on the sum of `cell_flags` on one device may be relied on, other than what follows from the above.
Results may differ from the reference program's by a relative error of at most 0.0012.
Values may be sent and summed in bfloat16 or wider, within the bound.
A program may use at most 128 MiB of HBM per device.

```python
import math
import jax
import jax.numpy as jnp
from jax import lax

MODES = 4096
NY = 128
NX = 128


def set_ends(entries, key, least, largest):
    spot = [jax.random.randint(jax.random.fold_in(key, axis), (), 0, length) for axis, length in enumerate(entries.shape)]
    longest = entries.shape.index(max(entries.shape))
    beside = spot[:longest] + [(spot[longest] + 1) % entries.shape[longest]] + spot[longest + 1:]
    return entries.at[tuple(spot)].set(least).at[tuple(beside)].set(largest)


def level_of(key, shape, cuts, low, high):
    level = 1.0
    for axis_at, shards_of in cuts:
        heights = jax.random.uniform(jax.random.fold_in(jax.random.fold_in(key, 6), axis_at), (shards_of,), jnp.float32, low / len(cuts), high / len(cuts))
        level = level * jnp.repeat(jnp.exp(heights), shape[axis_at] // shards_of).reshape((-1,) + (1,) * (len(shape) - 1 - axis_at))
    return level


def bell_draw(own_key, extent, scale, most, split=(), kind=jnp.bfloat16):
    level = level_of(own_key, extent, split, -0.22, 0.18) if split else 1.0
    entries = jax.random.normal(own_key, extent, jnp.float32) * scale * level
    return jnp.minimum(jnp.maximum(entries, -most), most).astype(kind)


def setup_inputs(seed: int = 0) -> dict:
    streams_of = jax.random.split(jax.random.key(seed), 6)
    return {
        "distribution": bell_draw(streams_of[0], (MODES, NX, NY), 1.0, 6.0, ((0, 8), (1, 16)), jnp.float32),
        "courant": jnp.clip(jax.random.uniform(streams_of[1], (2, MODES), jnp.float32, -0.4, 0.4) * level_of(streams_of[1], (2, MODES), ((1, 8),), -0.4, 0.0), -0.4, 0.4),
        "relax_rate": jnp.clip(jnp.exp(math.log(2.0) - 2.9957323 * jax.random.uniform(streams_of[2], (MODES,), jnp.float32) ** level_of(streams_of[2], (MODES,), ((0, 8),), -0.2, 0.2)), 0.1, 2.0),
        "scatter_weight": bell_draw(streams_of[3], (MODES, MODES), MODES ** -0.5, 0.09375, ((0, 8),), jnp.float32),
        "cell_flags": set_ends((jax.random.randint(streams_of[4], (NX, NY), 0, 4) < 1).astype(jnp.int32), jax.random.fold_in(streams_of[4], 1), 0, 1),
    }


time_step = 0.25
wall_rate = 2.0


def transport_rows(padded, cx, cy):
    full = jnp.pad(padded, ((0, 0), (0, 0), (2, 2)))
    centre = full[:, 2:-2, 2:-2]
    back_x = 1.5 * centre - 2.0 * full[:, 1:-3, 2:-2] + 0.5 * full[:, :-4, 2:-2]
    fwd_x = -1.5 * centre + 2.0 * full[:, 3:-1, 2:-2] - 0.5 * full[:, 4:, 2:-2]
    back_y = 1.5 * centre - 2.0 * full[:, 2:-2, 1:-3] + 0.5 * full[:, 2:-2, :-4]
    fwd_y = -1.5 * centre + 2.0 * full[:, 2:-2, 3:-1] - 0.5 * full[:, 2:-2, 4:]
    return (jnp.maximum(cx, 0.0) * back_x + jnp.minimum(cx, 0.0) * fwd_x
            + jnp.maximum(cy, 0.0) * back_y + jnp.minimum(cy, 0.0) * fwd_y)


def advance(field, courant, relax_rate, scatter_weight, flags):
    cx = courant[0][:, None, None]
    cy = courant[1][:, None, None]
    padded = jnp.pad(field, ((0, 0), (2, 2), (0, 0)))
    moved = transport_rows(padded, cx, cy)
    rounded = field.astype(jnp.bfloat16).reshape(field.shape[0], -1).astype(jnp.float32)
    gain = jnp.dot(scatter_weight, rounded, precision=lax.Precision.HIGHEST,
                   preferred_element_type=jnp.float32).reshape(field.shape)
    rate = relax_rate[:, None, None]
    return field - moved + time_step * (gain - rate * field - wall_rate * flags * field)


def reference(distribution, courant, relax_rate, scatter_weight, cell_flags):
    flags = cell_flags.astype(jnp.float32)[None]
    first = advance(distribution, courant, relax_rate, scatter_weight, flags)
    return advance(first, courant, relax_rate, scatter_weight, flags)
```

```python
import jax
import jax.numpy as jnp
from jax import lax
from jax.experimental import pallas as pl
from jax.experimental.pallas import tpu as pltpu
from jax.sharding import PartitionSpec as P

MESH = pl.DeviceIdType.MESH
f32 = jnp.float32
bf16 = jnp.bfloat16
MB = 512
NC = 128
ROWS = 8
NMODES = 4096
STAGE = 128
WU = 4
WR = 16
TOP = 31000.0


def kernel(dist, courant, rate, flags, weight, out,
           X, Fs, G, Cs, Cr, B, Wb, Wlo, Wst, Wsf, Wsh, coef, acc, wall, D,
           lsem, sx, rx, sz, rz, sf, rf, sc, rc, sh, rh,
           swx, rwx, swy, rwy, swf, rwf, swp, rwp):
    mi = lax.axis_index("mode")
    ti = lax.axis_index("tile")
    h, z = mi // 4, mi % 4
    y, l, c = ti // 4, (ti // 2) % 2, ti % 2

    def dev(h_, z_, y_, l_, c_):
        return (h_ * 4 + z_, y_ * 4 + l_ * 2 + c_)

    zp, zm, zz = (z + 1) % 4, (z + 3) % 4, (z + 2) % 4
    yp, ym, yy = (y + 1) % 4, (y + 3) % 4, (y + 2) % 4
    Ns = dev(h, z, y, 1 - l, c)
    No = dev(1 - h, z, y, 1 - l, c)
    Zp, Zm = dev(h, zp, y, l, c), dev(h, zm, y, l, c)
    Yp, Ym = dev(h, z, yp, l, c), dev(h, z, ym, l, c)
    Pc = dev(h, z, y, l, 1 - c)
    Hn, Hp = (mi, (ti + 1) % 16), (mi, (ti + 15) % 16)
    side = 1 - (h + l) % 2
    half_of = (1 - side, side)
    nbr = (Ns, No)
    hof = (h, 1 - h)
    q = y * 2 + c

    def row(half, j):
        return 3 - j + half * (1 + 2 * j)

    def rcopy(src, dst, ssem, rsem, to):
        return pltpu.make_async_remote_copy(
            src_ref=src, dst_ref=dst, send_sem=ssem, recv_sem=rsem,
            device_id=to, device_id_type=MESH)

    def cx(t, j, k):
        n = t * 4 + j
        return rcopy(Fs.at[t, row(half_of[k], j)], G.at[n, h * 4 + z],
                     sx.at[n, k], rx.at[n, k], nbr[k])

    def cx_in(n, k):
        blk = G.at[n, hof[k] * 4 + z]
        return rcopy(blk, blk, sx.at[n, k], rx.at[n, k], nbr[k])

    def cz(n, k, way):
        blk = G.at[n, hof[k] * 4 + z]
        return rcopy(blk, blk, sz.at[n, k, way], rz.at[n, k, way], (Zp, Zm)[way])

    def cz_in(n, k, way):
        blk = G.at[n, hof[k] * 4 + (zm, zp)[way]]
        return rcopy(blk, blk, sz.at[n, k, way], rz.at[n, k, way], (Zp, Zm)[way])

    def cf(n, way):
        blk = G.at[n, hof[way] * 4 + (zm, zp)[way]]
        return rcopy(blk, blk, sf.at[n, way], rf.at[n, way], (Zp, Zm)[way])

    def cf_in(n, way):
        blk = G.at[n, hof[way] * 4 + zz]
        return rcopy(blk, blk, sf.at[n, way], rf.at[n, way], (Zp, Zm)[way])

    def cc(n, k):
        return rcopy(Cs.at[n, k], Cr.at[n, k], sc.at[n, k], rc.at[n, k], nbr[k])

    def ch(t, d, way):
        src, dst = ((8 + d, d), (3 - d, 11 - d))[way]
        return rcopy(X.at[t, src], X.at[t, dst], sh.at[t, d, way], rh.at[t, d, way], (Hn, Hp)[way])

    def wrow(y_, c_, u):
        return Wb.at[1, (y_ * 2 + c_) * WU + u]

    def cwx(u):
        return rcopy(Wsh.at[u], wrow(y, c, u), swx.at[u], rwx.at[u], No)

    def cwy(u, way):
        blk = wrow(y, c, u)
        return rcopy(blk, blk, swy.at[u, way], rwy.at[u, way], (Yp, Ym)[way])

    def cwy_in(u, way):
        blk = wrow((ym, yp)[way], c, u)
        return rcopy(blk, blk, swy.at[u, way], rwy.at[u, way], (Yp, Ym)[way])

    def cwf(u):
        way = u % 2
        blk = wrow((ym, yp)[way], c, u)
        return rcopy(blk, blk, swf.at[u], rwf.at[u], (Yp, Ym)[way])

    def cwf_in(u):
        blk = wrow(yy, c, u)
        return rcopy(blk, blk, swf.at[u], rwf.at[u], (Yp, Ym)[u % 2])

    def cwp(y_, u):
        blk = wrow(y_, c, u)
        return rcopy(blk, blk, swp.at[y_, u], rwp.at[y_, u], Pc)

    def cwp_in(y_, u):
        blk = wrow(y_, 1 - c, u)
        return rcopy(blk, blk, swp.at[y_, u], rwp.at[y_, u], Pc)

    load_d = pltpu.make_async_copy(dist, D, lsem.at[0])
    load_s = pltpu.make_async_copy(weight.at[pl.ds(q * 64, 64)], Wsf, lsem.at[1])
    load_d.start()
    load_s.start()

    def load_w(i):
        return pltpu.make_async_copy(
            weight.at[pl.ds(i * STAGE, STAGE)], Wst.at[i % 2], lsem.at[2 + i % 2])

    load_w(0).start()
    load_w(1).start()

    barrier = pltpu.get_barrier_semaphore()
    for to in (Ns, No, Zp, Zm, Yp, Ym, Pc, Hn, Hp):
        pl.semaphore_signal(barrier, inc=1, device_id=to, device_id_type=MESH)
    pl.semaphore_wait(barrier, 9)

    load_d.wait()

    def take(r):
        v = D[pl.ds(r, MB, stride=ROWS), :]
        X[0, 2 + r] = v
        Fs[0, r] = v.astype(bf16)

    def first_send(j):
        take(3 - j)
        take(4 + j)
        cx(0, j, 0).start()
        cx(0, j, 1).start()

    shared = []

    def share(u):
        if not shared:
            load_s.wait()
        shared.append(u)
        Wsh[u] = Wsf[pl.ds(u * WR, WR), :].astype(bf16)
        cwx(u).start()

    def halo(t, d):
        ch(t, d, 0).start()
        ch(t, d, 1).start()

    def zown(n, k):
        cx_in(n, k).wait_recv()
        cz(n, k, 0).start()
        cz(n, k, 1).start()

    def zfwd(n, k):
        cz_in(n, k, k).wait_recv()
        cf(n, k).start()

    def cast_w(i):
        load_w(i).wait()

        @pl.loop(0, STAGE // WR)
        def _(r):
            v = Wst[i % 2, pl.ds(r * WR, WR), :]
            high_part = v.astype(bf16)
            Wb[0, i * (STAGE // WR) + r] = high_part
            Wlo[i * (STAGE // WR) + r] = (v - high_part.astype(f32)).astype(bf16)

        if i + 2 < MB // STAGE:
            load_w(i + 2).start()

    def w1(u):
        cwx(u).wait_recv()
        cwy(u, 0).start()
        cwy(u, 1).start()
        cwp(y, u).start()

    def w2(u, way):
        cwy_in(u, way).wait_recv()
        if u % 2 == way:
            cwf(u).start()
        cwp((ym, yp)[way], u).start()

    def w3(u):
        cwf_in(u).wait_recv()
        cwp(yy, u).start()

    def wfin():
        for u in range(WU):
            for y_ in (y, ym, yp, yy):
                cwp_in(y_, u).wait_recv()

    def coefs():
        for r in range(ROWS):
            wall[r] = jnp.broadcast_to(0.5 * flags[r:r + 1, :].astype(f32), (8, NC))
        for i in range(MB // NC):
            at = pl.ds(i * NC, NC)
            for k, line in ((0, courant[0:1, at]), (1, courant[1:2, at]), (2, rate[0:1, at])):
                coef[k, at, :] = jnp.transpose(jnp.broadcast_to(line, (NC, NC)))

    low = jnp.where(ti > 0, 1.0, 0.0).astype(f32)
    high = jnp.where(ti < 15, 1.0, 0.0).astype(f32)

    def base(t, edge):
        if edge:
            for d in (0, 1):
                ch(t, d, 0).wait_recv()
                ch(t, d, 1).wait_recv()
        rows = (0, 1, 6, 7) if edge else (2, 3, 4, 5)
        used = sorted({r + d for r in rows for d in range(5)})
        lane = lax.broadcasted_iota(jnp.int32, (8, NC), 1)

        def modes(g):
            at = pl.ds(pl.multiple_of(g * 8, 8), 8)
            vx, vy, rt = coef[0, at, :], coef[1, at, :], coef[2, at, :]
            px, nx = jnp.maximum(vx, 0.0), jnp.minimum(vx, 0.0)
            py, ny = jnp.maximum(vy, 0.0), jnp.minimum(vy, 0.0)
            diag = 1.0 - 1.5 * ((px - nx) + (py - ny)) - 0.25 * rt
            a1, a2, b1, b2 = 2.0 * px, -0.5 * px, -2.0 * nx, 0.5 * nx
            e1 = jnp.where(lane >= 1, 2.0 * py, 0.0)
            e2 = jnp.where(lane >= 2, -0.5 * py, 0.0)
            g1 = jnp.where(lane < NC - 1, -2.0 * ny, 0.0)
            g2 = jnp.where(lane < NC - 2, 0.5 * ny, 0.0)
            x = {r: X[t, r, at, :] for r in used}
            if edge:
                x[0], x[1] = x[0] * low, x[1] * low
                x[10], x[11] = x[10] * high, x[11] * high
            for r in rows:
                f = x[r + 2]
                v = f * (diag - wall[r])
                v = v + a1 * x[r + 1] + a2 * x[r] + b1 * x[r + 3] + b2 * x[r + 4]
                v = v + e1 * pltpu.roll(f, 1, 1) + e2 * pltpu.roll(f, 2, 1)
                v = v + g1 * pltpu.roll(f, NC - 1, 1) + g2 * pltpu.roll(f, NC - 2, 1)
                B[r, at, :] = v

        @pl.loop(0, MB // 32)
        def _(g):
            for i in range(4):
                modes(g * 4 + i)

    def ship(n, k, v):
        top = jnp.maximum(jnp.max(jnp.abs(v), axis=0, keepdims=True), 1e-20)
        power = jnp.ceil(jnp.log2(top))
        code = jnp.round(v * (jnp.exp2(-power) * TOP))
        Cs[n, k, 0:MB, :] = code.astype(jnp.int32).astype(jnp.int16)
        Cs[n, k, MB:MB + 16, :] = jnp.broadcast_to(power, (16, NC)).astype(jnp.int32).astype(jnp.int16)
        cc(n, k).start()

    def quarter(n, k):
        power = Cr[n, k, MB:MB + 16, :].astype(jnp.int32).astype(f32)[0:1, :]
        return Cr[n, k, 0:MB, :].astype(jnp.int32).astype(f32) * (jnp.exp2(power) * (0.25 / TOP))

    parts = (lambda at: (Wb[0, :, :, at], Wlo[:, :, at]), lambda at: (Wb[1, :, :, at],))

    def times(w, at, g):
        total = None
        for part in parts[w](at):
            term = jnp.dot(part.reshape(MB, -1), g, preferred_element_type=f32)
            total = term if total is None else total + term
        return total

    def gain(w, *ns):
        if w == 0:
            for n in ns:
                for k in (0, 1):
                    cz_in(n, k, 1 - k).wait_recv()
                    cf_in(n, k).wait_recv()
        cells = [G[n].reshape(NMODES, NC) for n in ns]
        cells = cells[0] if len(ns) == 1 else jnp.concatenate(cells, axis=1)
        acc[:, 0:len(ns) * NC] = times(w, slice(None), cells)
        for i, n in enumerate(ns):
            ship(n, w, acc[:, i * NC:(i + 1) * NC])

    def layer(w, n, z_):
        at = [pl.ds(pl.multiple_of(hh * 4 * MB + z_ * MB, MB), MB) for hh in (0, 1)]
        cells = [G[n, z_], G[n, 4 + z_]]
        terms = list(zip(*(parts[w](a) for a in at)))
        left = [v.reshape(MB, MB) for term in terms for v in term]
        return jnp.dot(jnp.concatenate(left, axis=1), jnp.concatenate(cells * len(terms), axis=0),
                       preferred_element_type=f32)

    def early(n):
        cz_in(n, 0, 1).wait_recv()
        cz_in(n, 1, 0).wait_recv()
        for w in (0, 1):
            at = pl.ds(w * NC, NC)
            acc[:, at] = layer(w, n, z)

            @pl.loop(0, 2)
            def _(i):
                acc[:, at] += layer(w, n, (z + 1 + 2 * i) % 4)

    def late(n, w):
        if w == 0:
            cf_in(n, 0).wait_recv()
            cf_in(n, 1).wait_recv()
        ship(n, w, acc[:, w * NC:(w + 1) * NC] + layer(w, n, zz))

    def u1(j, k):
        cc(j, k).wait_recv()
        r = row(half_of[k], j)
        v = B[r] + quarter(j, k)
        X[1, 2 + r] = v
        Fs[1, r] = v.astype(bf16)
        cx(1, j, k).start()

    def u2(j):
        n = 4 + j
        cc(n, 0).wait_recv()
        cc(n, 1).wait_recv()
        at0 = half_of[0]
        D[pl.ds(3 - j, MB, stride=ROWS), :] = B[3 - j] + quarter(n, at0)
        D[pl.ds(4 + j, MB, stride=ROWS), :] = B[4 + j] + quarter(n, 1 - at0)

    share(1)
    share(2)
    first_send(0)
    cast_w(0)
    first_send(1)
    cast_w(1)
    share(0)
    share(3)
    w1(1)
    zown(0, 0)
    w1(2)
    first_send(2)
    zown(1, 0)
    coefs()
    first_send(3)
    cast_w(2)
    zown(0, 1)
    halo(0, 0)
    w2(1, 1)
    w2(2, 0)
    zown(1, 1)
    zfwd(0, 0)
    cast_w(3)
    w1(0)
    zfwd(1, 0)
    zfwd(0, 1)
    w1(3)
    zfwd(1, 1)
    w2(2, 1)
    w2(0, 1)
    w3(1)
    zown(2, 0)
    zown(3, 0)
    w2(0, 0)
    base(0, 0)
    w2(3, 0)
    w2(3, 1)
    gain(0, 0, 1)
    w3(0)
    zown(3, 1)
    w3(2)
    zfwd(2, 0)
    w2(1, 0)
    zown(2, 1)
    w3(3)
    wfin()
    gain(1, 0, 1)
    zfwd(3, 0)
    zfwd(3, 1)
    u1(0, 0)
    u1(1, 0)
    zfwd(2, 1)
    halo(0, 1)
    zown(4, 0)
    u1(0, 1)
    u1(1, 1)
    zown(5, 0)
    gain(0, 2, 3)
    zown(4, 1)
    gain(1, 2, 3)
    zown(5, 1)
    zfwd(5, 0)
    base(0, 1)
    zfwd(4, 1)
    zfwd(4, 0)
    u1(2, 0)
    zfwd(5, 1)
    u1(2, 1)
    u1(3, 0)
    zown(6, 0)
    zown(6, 1)
    u1(3, 1)
    halo(1, 1)
    zown(7, 0)
    gain(0, 4, 5)
    halo(1, 0)
    zfwd(6, 1)
    zfwd(6, 0)
    gain(1, 4, 5)
    zown(7, 1)
    zfwd(7, 0)
    base(1, 0)
    gain(0, 6)
    zfwd(7, 1)
    gain(1, 6)
    early(7)
    late(7, 0)
    late(7, 1)
    u2(1)
    base(1, 1)
    u2(0)
    u2(2)
    u2(3)
    store = pltpu.make_async_copy(D, out, lsem.at[0])
    store.start()

    for t in (0, 1):
        for k in (0, 1):
            ch(t, 0, k).wait_send()
            ch(t, 1, k).wait_send()
        for j in range(4):
            for k in (0, 1):
                cx(t, j, k).wait_send()
    for n in range(8):
        for k in (0, 1):
            cz(n, 0, k).wait_send()
            cz(n, 1, k).wait_send()
            cf(n, k).wait_send()
            cc(n, k).wait_send()
    for u in range(WU):
        cwx(u).wait_send()
        cwy(u, 0).wait_send()
        cwy(u, 1).wait_send()
        cwf(u).wait_send()
        for y_ in range(4):
            cwp(y_, u).wait_send()
    store.wait()


def body(distribution, courant, relax_rate, scatter_weight, cell_flags):
    vmem = pl.BlockSpec(memory_space=pltpu.VMEM)
    hbm = pl.BlockSpec(memory_space=pl.ANY)
    dma = pltpu.SemaphoreType.DMA
    out = pl.pallas_call(
        kernel,
        out_shape=jax.ShapeDtypeStruct((MB * ROWS, NC), f32),
        in_specs=[hbm, vmem, vmem, vmem, hbm],
        out_specs=hbm,
        scratch_shapes=[
            pltpu.VMEM((2, 12, MB, NC), f32),
            pltpu.VMEM((2, ROWS, MB, NC), bf16),
            pltpu.VMEM((8, 8, MB, NC), bf16),
            pltpu.VMEM((8, 2, MB + 16, NC), jnp.int16),
            pltpu.VMEM((8, 2, MB + 16, NC), jnp.int16),
            pltpu.VMEM((ROWS, MB, NC), f32),
            pltpu.VMEM((2, MB // WR, WR, NMODES), bf16),
            pltpu.VMEM((MB // WR, WR, NMODES), bf16),
            pltpu.VMEM((2, STAGE, NMODES), f32),
            pltpu.VMEM((64, NMODES), f32),
            pltpu.VMEM((WU, WR, NMODES), bf16),
            pltpu.VMEM((3, MB, NC), f32),
            pltpu.VMEM((MB, 2 * NC), f32),
            pltpu.VMEM((ROWS, 8, NC), f32),
            pltpu.VMEM((MB * ROWS, NC), f32),
            dma((4,)),
            dma((8, 2)), dma((8, 2)),
            dma((8, 2, 2)), dma((8, 2, 2)),
            dma((8, 2)), dma((8, 2)),
            dma((8, 2)), dma((8, 2)),
            dma((2, 2, 2)), dma((2, 2, 2)),
            dma((WU,)), dma((WU,)),
            dma((WU, 2)), dma((WU, 2)),
            dma((WU,)), dma((WU,)),
            dma((4, WU)), dma((4, WU)),
        ],
        compiler_params=pltpu.CompilerParams(
            collective_id=0, has_side_effects=True, vmem_limit_bytes=60 * 1024 * 1024),
    )(distribution.reshape(MB * ROWS, NC), courant, relax_rate.reshape(1, MB),
      cell_flags, scatter_weight)
    return out.reshape(distribution.shape)


def solution(mesh):
    in_specs = (
        P("mode", "tile", None),
        P(None, "mode"),
        P("mode"),
        P("mode", None),
        P("tile", None),
    )
    out_specs = P("mode", "tile", None)
    return jax.shard_map(body, mesh=mesh, in_specs=in_specs, out_specs=out_specs, check_vma=False)
```

```python
import jax
import jax.numpy as jnp
from jax import lax
from jax.experimental import pallas as pl
from jax.experimental.pallas import tpu as pltpu
from jax.sharding import PartitionSpec as P

MESH = pl.DeviceIdType.MESH
f32 = jnp.float32
bf16 = jnp.bfloat16
MB = 512
NC = 128
ROWS = 8
NMODES = 4096
STAGE = 128
WU = 4
WR = 16
TOP = 31000.0


def kernel(dist, courant, rate, flags, weight, out,
           X, Fs, G, Cs, Cr, B, Wb, Wlo, Wst, Wsf, Wsh, coef, acc, wall, D,
           lsem, sx, rx, sz, rz, sf, rf, sc, rc, sh, rh,
           swx, rwx, swy, rwy, swf, rwf, swp, rwp):
    mi = lax.axis_index("mode")
    ti = lax.axis_index("tile")
    h, z = mi // 4, mi % 4
    y, l, c = ti // 4, (ti // 2) % 2, ti % 2

    def dev(h_, z_, y_, l_, c_):
        return (h_ * 4 + z_, y_ * 4 + l_ * 2 + c_)

    zp, zm, zz = (z + 1) % 4, (z + 3) % 4, (z + 2) % 4
    yp, ym, yy = (y + 1) % 4, (y + 3) % 4, (y + 2) % 4
    Ns = dev(h, z, y, 1 - l, c)
    No = dev(1 - h, z, y, 1 - l, c)
    Zp, Zm = dev(h, zp, y, l, c), dev(h, zm, y, l, c)
    Yp, Ym = dev(h, z, yp, l, c), dev(h, z, ym, l, c)
    Pc = dev(h, z, y, l, 1 - c)
    Hn, Hp = (mi, (ti + 1) % 16), (mi, (ti + 15) % 16)
    side = 1 - (h + l) % 2
    half_of = (1 - side, side)
    nbr = (Ns, No)
    hof = (h, 1 - h)
    q = y * 2 + c

    def row(half, j):
        return 3 - j + half * (1 + 2 * j)

    def rcopy(src, dst, ssem, rsem, to):
        return pltpu.make_async_remote_copy(
            src_ref=src, dst_ref=dst, send_sem=ssem, recv_sem=rsem,
            device_id=to, device_id_type=MESH)

    def cx(t, j, k):
        n = t * 4 + j
        return rcopy(Fs.at[t, row(half_of[k], j)], G.at[n, h * 4 + z],
                     sx.at[n, k], rx.at[n, k], nbr[k])

    def cx_in(n, k):
        blk = G.at[n, hof[k] * 4 + z]
        return rcopy(blk, blk, sx.at[n, k], rx.at[n, k], nbr[k])

    def cz(n, k, way):
        blk = G.at[n, hof[k] * 4 + z]
        return rcopy(blk, blk, sz.at[n, k, way], rz.at[n, k, way], (Zp, Zm)[way])

    def cz_in(n, k, way):
        blk = G.at[n, hof[k] * 4 + (zm, zp)[way]]
        return rcopy(blk, blk, sz.at[n, k, way], rz.at[n, k, way], (Zp, Zm)[way])

    def cf(n, way):
        blk = G.at[n, hof[way] * 4 + (zm, zp)[way]]
        return rcopy(blk, blk, sf.at[n, way], rf.at[n, way], (Zp, Zm)[way])

    def cf_in(n, way):
        blk = G.at[n, hof[way] * 4 + zz]
        return rcopy(blk, blk, sf.at[n, way], rf.at[n, way], (Zp, Zm)[way])

    def cc(n, k):
        return rcopy(Cs.at[n, k], Cr.at[n, k], sc.at[n, k], rc.at[n, k], nbr[k])

    def ch(t, d, way):
        src, dst = ((8 + d, d), (3 - d, 11 - d))[way]
        return rcopy(X.at[t, src], X.at[t, dst], sh.at[t, d, way], rh.at[t, d, way], (Hn, Hp)[way])

    def wrow(y_, c_, u):
        return Wb.at[1, (y_ * 2 + c_) * WU + u]

    def cwx(u):
        return rcopy(Wsh.at[u], wrow(y, c, u), swx.at[u], rwx.at[u], No)

    def cwy(u, way):
        blk = wrow(y, c, u)
        return rcopy(blk, blk, swy.at[u, way], rwy.at[u, way], (Yp, Ym)[way])

    def cwy_in(u, way):
        blk = wrow((ym, yp)[way], c, u)
        return rcopy(blk, blk, swy.at[u, way], rwy.at[u, way], (Yp, Ym)[way])

    def cwf(u):
        way = u % 2
        blk = wrow((ym, yp)[way], c, u)
        return rcopy(blk, blk, swf.at[u], rwf.at[u], (Yp, Ym)[way])

    def cwf_in(u):
        blk = wrow(yy, c, u)
        return rcopy(blk, blk, swf.at[u], rwf.at[u], (Yp, Ym)[u % 2])

    def cwp(y_, u):
        blk = wrow(y_, c, u)
        return rcopy(blk, blk, swp.at[y_, u], rwp.at[y_, u], Pc)

    def cwp_in(y_, u):
        blk = wrow(y_, 1 - c, u)
        return rcopy(blk, blk, swp.at[y_, u], rwp.at[y_, u], Pc)

    load_d = pltpu.make_async_copy(dist, D, lsem.at[0])
    load_s = pltpu.make_async_copy(weight.at[pl.ds(q * 64, 64)], Wsf, lsem.at[1])
    load_d.start()
    load_s.start()

    def load_w(i):
        return pltpu.make_async_copy(
            weight.at[pl.ds(i * STAGE, STAGE)], Wst.at[i % 2], lsem.at[2 + i % 2])

    load_w(0).start()
    load_w(1).start()

    barrier = pltpu.get_barrier_semaphore()
    for to in (Ns, No, Zp, Zm, Yp, Ym, Pc, Hn, Hp):
        pl.semaphore_signal(barrier, inc=1, device_id=to, device_id_type=MESH)
    load_d.wait()

    def take(r):
        v = D[pl.ds(r, MB, stride=ROWS), :]
        X[0, 2 + r] = v
        Fs[0, r] = v.astype(bf16)

    def first_send(j):
        cx(0, j, 0).start()
        cx(0, j, 1).start()

    def share(u):
        cwx(u).start()

    def halo(t, d):
        ch(t, d, 0).start()
        ch(t, d, 1).start()

    for r in (3, 4, 2, 5, 1, 6, 0, 7):
        take(r)
    load_s.wait()
    for u in range(WU):
        Wsh[u] = Wsf[pl.ds(u * WR, WR), :].astype(bf16)
    def cast_w(i):
        load_w(i).wait()

        @pl.loop(0, STAGE // WR)
        def _(r):
            v = Wst[i % 2, pl.ds(r * WR, WR), :]
            high_part = v.astype(bf16)
            Wb[0, i * (STAGE // WR) + r] = high_part
            Wlo[i * (STAGE // WR) + r] = (v - high_part.astype(f32)).astype(bf16)

        if i + 2 < MB // STAGE:
            load_w(i + 2).start()

    def coefs():
        for r in range(ROWS):
            wall[r] = jnp.broadcast_to(0.5 * flags[r:r + 1, :].astype(f32), (8, NC))
        for i in range(MB // NC):
            at = pl.ds(i * NC, NC)
            vx, vy, rt = (jnp.transpose(jnp.broadcast_to(line, (NC, NC)))
                          for line in (courant[0:1, at], courant[1:2, at], rate[0:1, at]))
            lane = lax.broadcasted_iota(jnp.int32, (NC, NC), 1)
            ax = jnp.abs(vx)
            py, ny = jnp.maximum(vy, 0.0), jnp.minimum(vy, 0.0)
            coef[0, at, :] = vx
            coef[1, at, :] = 1.0 - 1.5 * (ax + jnp.abs(vy)) - 0.25 * rt
            coef[2, at, :] = 2.0 * ax
            coef[3, at, :] = -0.5 * ax
            coef[4, at, :] = jnp.where(lane >= 1, 2.0 * py, 0.0)
            coef[5, at, :] = jnp.where(lane >= 2, -0.5 * py, 0.0)
            coef[6, at, :] = jnp.where(lane < NC - 1, -2.0 * ny, 0.0)
            coef[7, at, :] = jnp.where(lane < NC - 2, 0.5 * ny, 0.0)

    for i in range(MB // STAGE):
        cast_w(i)
    coefs()
    pl.semaphore_wait(barrier, 9)

    def zown(n, k):
        cx_in(n, k).wait_recv()
        cz(n, k, 0).start()
        cz(n, k, 1).start()

    def zfwd(n, k):
        cz_in(n, k, k).wait_recv()
        cf(n, k).start()

    def w1(u):
        cwx(u).wait_recv()
        cwy(u, 0).start()
        cwy(u, 1).start()
        cwp(y, u).start()

    def w2(u, way):
        cwy_in(u, way).wait_recv()
        if u % 2 == way:
            cwf(u).start()
        cwp((ym, yp)[way], u).start()

    def w3(u):
        cwf_in(u).wait_recv()
        cwp(yy, u).start()

    def wfin():
        for u in range(WU):
            for y_ in (y, ym, yp, yy):
                cwp_in(y_, u).wait_recv()

    low = jnp.where(ti > 0, 1.0, 0.0).astype(f32)
    high = jnp.where(ti < 15, 1.0, 0.0).astype(f32)

    def base(t, edge):
        if edge:
            for d in (0, 1):
                ch(t, d, 0).wait_recv()
                ch(t, d, 1).wait_recv()
        rows = (0, 1, 6, 7) if edge else (2, 3, 4, 5)
        used = sorted({r + d for r in rows for d in range(5)})

        def modes(g):
            at = pl.ds(pl.multiple_of(g * 8, 8), 8)
            vx, diag, a1, a2, e1, e2, g1, g2 = (coef[i, at, :] for i in range(8))
            up = vx > 0.0
            x = {r: X[t, r, at, :] for r in used}
            if edge:
                x[0], x[1] = x[0] * low, x[1] * low
                x[10], x[11] = x[10] * high, x[11] * high
            for r in rows:
                f = x[r + 2]
                v = f * (diag - wall[r])
                v = v + a1 * jnp.where(up, x[r + 1], x[r + 3]) + a2 * jnp.where(up, x[r], x[r + 4])
                v = v + e1 * pltpu.roll(f, 1, 1) + e2 * pltpu.roll(f, 2, 1)
                v = v + g1 * pltpu.roll(f, NC - 1, 1) + g2 * pltpu.roll(f, NC - 2, 1)
                B[r, at, :] = v

        @pl.loop(0, MB // 64)
        def _(g):
            for i in range(8):
                modes(g * 8 + i)

    def ship(n, k, v):
        top = jnp.maximum(jnp.max(jnp.abs(v), axis=0, keepdims=True), 1e-20)
        power = jnp.ceil(jnp.log2(top))
        code = jnp.round(v * (jnp.exp2(-power) * TOP))
        Cs[n, k, 0:MB, :] = code.astype(jnp.int32).astype(jnp.int16)
        Cs[n, k, MB:MB + 16, :] = jnp.broadcast_to(power, (16, NC)).astype(jnp.int32).astype(jnp.int16)
        cc(n, k).start()

    def quarter(n, k):
        power = Cr[n, k, MB:MB + 16, :].astype(jnp.int32).astype(f32)[0:1, :]
        return Cr[n, k, 0:MB, :].astype(jnp.int32).astype(f32) * (jnp.exp2(power) * (0.25 / TOP))

    parts = (lambda at: (Wb[0, :, :, at], Wlo[:, :, at]), lambda at: (Wb[1, :, :, at],))

    def times(w, at, g):
        total = None
        for part in parts[w](at):
            term = jnp.dot(part.reshape(MB, -1), g, preferred_element_type=f32)
            total = term if total is None else total + term
        return total

    def gain(w, *ns):
        if w == 0:
            for n in ns:
                for k in (0, 1):
                    cz_in(n, k, 1 - k).wait_recv()
                    cf_in(n, k).wait_recv()
        cells = [G[n].reshape(NMODES, NC) for n in ns]
        cells = cells[0] if len(ns) == 1 else jnp.concatenate(cells, axis=1)
        acc[:, 0:len(ns) * NC] = times(w, slice(None), cells)
        for i, n in enumerate(ns):
            ship(n, w, acc[:, i * NC:(i + 1) * NC])

    def layer(w, n, z_):
        at = [pl.ds(pl.multiple_of(hh * 4 * MB + z_ * MB, MB), MB) for hh in (0, 1)]
        cells = [G[n, z_], G[n, 4 + z_]]
        terms = list(zip(*(parts[w](a) for a in at)))
        left = [v.reshape(MB, MB) for term in terms for v in term]
        return jnp.dot(jnp.concatenate(left, axis=1), jnp.concatenate(cells * len(terms), axis=0),
                       preferred_element_type=f32)

    def early(n):
        cz_in(n, 0, 1).wait_recv()
        cz_in(n, 1, 0).wait_recv()
        for w in (0, 1):
            at = pl.ds(w * NC, NC)
            acc[:, at] = layer(w, n, z)

            @pl.loop(0, 2)
            def _(i):
                acc[:, at] += layer(w, n, (z + 1 + 2 * i) % 4)

    def late(n, w):
        if w == 0:
            cf_in(n, 0).wait_recv()
            cf_in(n, 1).wait_recv()
        ship(n, w, acc[:, w * NC:(w + 1) * NC] + layer(w, n, zz))

    def u1(j, k):
        cc(j, k).wait_recv()
        r = row(half_of[k], j)
        v = B[r] + quarter(j, k)
        X[1, 2 + r] = v
        Fs[1, r] = v.astype(bf16)
        cx(1, j, k).start()

    def u2(j):
        n = 4 + j
        cc(n, 0).wait_recv()
        cc(n, 1).wait_recv()
        at0 = half_of[0]
        D[pl.ds(3 - j, MB, stride=ROWS), :] = B[3 - j] + quarter(n, at0)
        D[pl.ds(4 + j, MB, stride=ROWS), :] = B[4 + j] + quarter(n, 1 - at0)

    share(1)
    share(0)
    first_send(0)
    first_send(1)
    share(3)
    share(2)
    w1(1)
    zown(0, 0)
    first_send(2)
    zown(1, 0)
    w1(0)
    first_send(3)
    zown(0, 1)
    halo(0, 0)
    zown(1, 1)
    zfwd(0, 0)
    w2(1, 1)
    w2(0, 0)
    w1(3)
    zfwd(0, 1)
    zfwd(1, 0)
    base(0, 0)
    zfwd(1, 1)
    w1(2)
    w2(3, 1)
    w3(0)
    w2(3, 0)
    zown(3, 0)
    zown(2, 1)
    w3(1)
    w2(2, 0)
    w2(0, 1)
    w2(1, 0)
    gain(0, 0, 1)
    w2(2, 1)
    zown(2, 0)
    zfwd(3, 0)
    zown(3, 1)
    w3(3)
    w3(2)
    zfwd(2, 1)
    wfin()
    gain(1, 0, 1)
    u1(0, 0)
    u1(1, 0)
    zfwd(3, 1)
    zfwd(2, 0)
    u1(0, 1)
    zown(4, 0)
    halo(0, 1)
    u1(1, 1)
    zown(5, 0)
    gain(0, 2, 3)
    zown(4, 1)
    gain(1, 2, 3)
    zown(5, 1)
    base(0, 1)
    u1(2, 0)
    zfwd(4, 1)
    zfwd(4, 0)
    zfwd(5, 1)
    u1(3, 0)
    zfwd(5, 0)
    u1(2, 1)
    u1(3, 1)
    zown(6, 0)
    halo(1, 1)
    base(1, 0)
    zown(6, 1)
    zown(7, 0)
    gain(0, 4, 5)
    zfwd(6, 1)
    zfwd(6, 0)
    gain(1, 4, 5)
    zown(7, 1)
    halo(1, 0)
    zfwd(7, 0)
    gain(0, 6)
    zfwd(7, 1)
    gain(1, 6)
    early(7)
    late(7, 0)
    late(7, 1)
    u2(1)
    base(1, 1)
    u2(2)
    u2(0)
    u2(3)
    store = pltpu.make_async_copy(D, out, lsem.at[0])
    store.start()

    for t in (0, 1):
        for k in (0, 1):
            ch(t, 0, k).wait_send()
            ch(t, 1, k).wait_send()
        for j in range(4):
            for k in (0, 1):
                cx(t, j, k).wait_send()
    for n in range(8):
        for k in (0, 1):
            cz(n, 0, k).wait_send()
            cz(n, 1, k).wait_send()
            cf(n, k).wait_send()
            cc(n, k).wait_send()
    for u in range(WU):
        cwx(u).wait_send()
        cwy(u, 0).wait_send()
        cwy(u, 1).wait_send()
        cwf(u).wait_send()
        for y_ in range(4):
            cwp(y_, u).wait_send()
    store.wait()


def body(distribution, courant, relax_rate, scatter_weight, cell_flags):
    vmem = pl.BlockSpec(memory_space=pltpu.VMEM)
    hbm = pl.BlockSpec(memory_space=pl.ANY)
    dma = pltpu.SemaphoreType.DMA
    out = pl.pallas_call(
        kernel,
        out_shape=jax.ShapeDtypeStruct((MB * ROWS, NC), f32),
        in_specs=[hbm, vmem, vmem, vmem, hbm],
        out_specs=hbm,
        scratch_shapes=[
            pltpu.VMEM((2, 12, MB, NC), f32),
            pltpu.VMEM((2, ROWS, MB, NC), bf16),
            pltpu.VMEM((8, 8, MB, NC), bf16),
            pltpu.VMEM((8, 2, MB + 16, NC), jnp.int16),
            pltpu.VMEM((8, 2, MB + 16, NC), jnp.int16),
            pltpu.VMEM((ROWS, MB, NC), f32),
            pltpu.VMEM((2, MB // WR, WR, NMODES), bf16),
            pltpu.VMEM((MB // WR, WR, NMODES), bf16),
            pltpu.VMEM((2, STAGE, NMODES), f32),
            pltpu.VMEM((64, NMODES), f32),
            pltpu.VMEM((WU, WR, NMODES), bf16),
            pltpu.VMEM((8, MB, NC), f32),
            pltpu.VMEM((MB, 2 * NC), f32),
            pltpu.VMEM((ROWS, 8, NC), f32),
            pltpu.VMEM((MB * ROWS, NC), f32),
            dma((4,)),
            dma((8, 2)), dma((8, 2)),
            dma((8, 2, 2)), dma((8, 2, 2)),
            dma((8, 2)), dma((8, 2)),
            dma((8, 2)), dma((8, 2)),
            dma((2, 2, 2)), dma((2, 2, 2)),
            dma((WU,)), dma((WU,)),
            dma((WU, 2)), dma((WU, 2)),
            dma((WU,)), dma((WU,)),
            dma((4, WU)), dma((4, WU)),
        ],
        compiler_params=pltpu.CompilerParams(
            collective_id=0, has_side_effects=True, vmem_limit_bytes=60 * 1024 * 1024),
    )(distribution.reshape(MB * ROWS, NC), courant, relax_rate.reshape(1, MB),
      cell_flags, scatter_weight)
    return out.reshape(distribution.shape)


def solution(mesh):
    in_specs = (
        P("mode", "tile", None),
        P(None, "mode"),
        P("mode"),
        P("mode", None),
        P("tile", None),
    )
    out_specs = P("mode", "tile", None)
    return jax.shard_map(body, mesh=mesh, in_specs=in_specs, out_specs=out_specs, check_vma=False)
```

```python
import jax
import jax.numpy as jnp
from jax import lax
from jax.experimental import pallas as pl
from jax.experimental.pallas import tpu as pltpu
from jax.sharding import PartitionSpec as P

MESH = pl.DeviceIdType.MESH
f32 = jnp.float32
bf16 = jnp.bfloat16
MB = 512
NC = 128
ROWS = 8
NMODES = 4096
STAGE = 128
WU = 4
WR = 16
TOP = 31000.0


def kernel(dist, courant, rate, flags, weight, out,
           X, Fs, G, Cs, Cr, B, Wb, Wst, Wsf, Wsh, coef, acc, wall, D,
           lsem, sx, rx, sz, rz, sf, rf, sc, rc, sh, rh,
           swx, rwx, swy, rwy, swf, rwf, swp, rwp):
    mi = lax.axis_index("mode")
    ti = lax.axis_index("tile")
    h, z = mi // 4, mi % 4
    y, l, c = ti // 4, (ti // 2) % 2, ti % 2

    def dev(h_, z_, y_, l_, c_):
        return (h_ * 4 + z_, y_ * 4 + l_ * 2 + c_)

    zp, zm, zz = (z + 1) % 4, (z + 3) % 4, (z + 2) % 4
    yp, ym, yy = (y + 1) % 4, (y + 3) % 4, (y + 2) % 4
    Ns = dev(h, z, y, 1 - l, c)
    No = dev(1 - h, z, y, 1 - l, c)
    Zp, Zm = dev(h, zp, y, l, c), dev(h, zm, y, l, c)
    Yp, Ym = dev(h, z, yp, l, c), dev(h, z, ym, l, c)
    Pc = dev(h, z, y, l, 1 - c)
    Hn, Hp = (mi, (ti + 1) % 16), (mi, (ti + 15) % 16)
    side = 1 - (h + l) % 2
    half_of = (1 - side, side)
    nbr = (Ns, No)
    hof = (h, 1 - h)
    q = y * 2 + c

    def row(half, j):
        return 3 - j + half * (1 + 2 * j)

    def rcopy(src, dst, ssem, rsem, to):
        return pltpu.make_async_remote_copy(
            src_ref=src, dst_ref=dst, send_sem=ssem, recv_sem=rsem,
            device_id=to, device_id_type=MESH)

    def cx(t, j, k):
        n = t * 4 + j
        return rcopy(Fs.at[t, row(half_of[k], j)], G.at[n, h * 4 + z],
                     sx.at[n, k], rx.at[n, k], nbr[k])

    def cx_in(n, k):
        blk = G.at[n, hof[k] * 4 + z]
        return rcopy(blk, blk, sx.at[n, k], rx.at[n, k], nbr[k])

    def cz(n, k, way):
        blk = G.at[n, hof[k] * 4 + z]
        return rcopy(blk, blk, sz.at[n, k, way], rz.at[n, k, way], (Zp, Zm)[way])

    def cz_in(n, k, way):
        blk = G.at[n, hof[k] * 4 + (zm, zp)[way]]
        return rcopy(blk, blk, sz.at[n, k, way], rz.at[n, k, way], (Zp, Zm)[way])

    def cf(n, way):
        blk = G.at[n, hof[way] * 4 + (zm, zp)[way]]
        return rcopy(blk, blk, sf.at[n, way], rf.at[n, way], (Zp, Zm)[way])

    def cf_in(n, way):
        blk = G.at[n, hof[way] * 4 + zz]
        return rcopy(blk, blk, sf.at[n, way], rf.at[n, way], (Zp, Zm)[way])

    def cc(n, k):
        return rcopy(Cs.at[n, k], Cr.at[n, k], sc.at[n, k], rc.at[n, k], nbr[k])

    def ch(t, d, way):
        src, dst = ((8 + d, d), (3 - d, 11 - d))[way]
        return rcopy(X.at[t, src], X.at[t, dst], sh.at[t, d, way], rh.at[t, d, way], (Hn, Hp)[way])

    def wrow(y_, c_, u):
        return Wb.at[1, (y_ * 2 + c_) * WU + u]

    def cwx(u):
        return rcopy(Wsh.at[u], wrow(y, c, u), swx.at[u], rwx.at[u], No)

    def cwy(u, way):
        blk = wrow(y, c, u)
        return rcopy(blk, blk, swy.at[u, way], rwy.at[u, way], (Yp, Ym)[way])

    def cwy_in(u, way):
        blk = wrow((ym, yp)[way], c, u)
        return rcopy(blk, blk, swy.at[u, way], rwy.at[u, way], (Yp, Ym)[way])

    def cwf(u):
        way = u % 2
        blk = wrow((ym, yp)[way], c, u)
        return rcopy(blk, blk, swf.at[u], rwf.at[u], (Yp, Ym)[way])

    def cwf_in(u):
        blk = wrow(yy, c, u)
        return rcopy(blk, blk, swf.at[u], rwf.at[u], (Yp, Ym)[u % 2])

    def cwp(y_, u):
        blk = wrow(y_, c, u)
        return rcopy(blk, blk, swp.at[y_, u], rwp.at[y_, u], Pc)

    def cwp_in(y_, u):
        blk = wrow(y_, 1 - c, u)
        return rcopy(blk, blk, swp.at[y_, u], rwp.at[y_, u], Pc)

    load_d = pltpu.make_async_copy(dist, D, lsem.at[0])
    load_s = pltpu.make_async_copy(weight.at[pl.ds(q * 64, 64)], Wsf, lsem.at[1])
    load_d.start()
    load_s.start()

    def load_w(i):
        return pltpu.make_async_copy(
            weight.at[pl.ds(i * STAGE, STAGE)], Wst.at[i % 2], lsem.at[2 + i % 2])

    load_w(0).start()
    load_w(1).start()

    barrier = pltpu.get_barrier_semaphore()
    for to in (Ns, No, Zp, Zm, Yp, Ym, Pc, Hn, Hp):
        pl.semaphore_signal(barrier, inc=1, device_id=to, device_id_type=MESH)
    pl.semaphore_wait(barrier, 9)

    load_d.wait()

    def take(r):
        v = D[pl.ds(r, MB, stride=ROWS), :]
        X[0, 2 + r] = v
        Fs[0, r] = v.astype(bf16)

    def first_send(j):
        take(3 - j)
        take(4 + j)
        cx(0, j, 0).start()
        cx(0, j, 1).start()

    shared = []

    def share(u):
        if not shared:
            load_s.wait()
        shared.append(u)
        Wsh[u] = Wsf[pl.ds(u * WR, WR), :].astype(bf16)
        cwx(u).start()

    def halo(t, d):
        ch(t, d, 0).start()
        ch(t, d, 1).start()

    def zown(n, k):
        cx_in(n, k).wait_recv()
        cz(n, k, 0).start()
        cz(n, k, 1).start()

    def zfwd(n, k):
        cz_in(n, k, k).wait_recv()
        cf(n, k).start()

    def cast_w(i):
        load_w(i).wait()

        @pl.loop(0, STAGE // WR)
        def _(r):
            v = Wst[i % 2, pl.ds(r * WR, WR), :]
            Wb[0, i * (STAGE // WR) + r] = v.astype(bf16)

        if i + 2 < MB // STAGE:
            load_w(i + 2).start()

    def w1(u):
        cwx(u).wait_recv()
        cwy(u, 0).start()
        cwy(u, 1).start()
        cwp(y, u).start()

    def w2(u, way):
        cwy_in(u, way).wait_recv()
        if u % 2 == way:
            cwf(u).start()
        cwp((ym, yp)[way], u).start()

    def w3(u):
        cwf_in(u).wait_recv()
        cwp(yy, u).start()

    def wfin():
        for u in range(WU):
            for y_ in (y, ym, yp, yy):
                cwp_in(y_, u).wait_recv()

    def coefs():
        for r in range(ROWS):
            wall[r] = jnp.broadcast_to(0.5 * flags[r:r + 1, :].astype(f32), (8, NC))
        for i in range(MB // NC):
            at = pl.ds(i * NC, NC)
            vx, vy, rt = (jnp.transpose(jnp.broadcast_to(line, (NC, NC)))
                          for line in (courant[0:1, at], courant[1:2, at], rate[0:1, at]))
            lane = lax.broadcasted_iota(jnp.int32, (NC, NC), 1)
            ax = jnp.abs(vx)
            py, ny = jnp.maximum(vy, 0.0), jnp.minimum(vy, 0.0)
            coef[0, at, :] = vx
            coef[1, at, :] = 1.0 - 1.5 * (ax + jnp.abs(vy)) - 0.25 * rt
            coef[2, at, :] = 2.0 * ax
            coef[3, at, :] = -0.5 * ax
            coef[4, at, :] = jnp.where(lane >= 1, 2.0 * py, 0.0)
            coef[5, at, :] = jnp.where(lane >= 2, -0.5 * py, 0.0)
            coef[6, at, :] = jnp.where(lane < NC - 1, -2.0 * ny, 0.0)
            coef[7, at, :] = jnp.where(lane < NC - 2, 0.5 * ny, 0.0)

    low = jnp.where(ti > 0, 1.0, 0.0).astype(f32)
    high = jnp.where(ti < 15, 1.0, 0.0).astype(f32)

    def base(t, edge):
        if edge:
            for d in (0, 1):
                ch(t, d, 0).wait_recv()
                ch(t, d, 1).wait_recv()
        rows = (0, 1, 6, 7) if edge else (2, 3, 4, 5)
        used = sorted({r + d for r in rows for d in range(5)})

        def modes(g):
            at = pl.ds(pl.multiple_of(g * 8, 8), 8)
            vx, diag, a1, a2, e1, e2, g1, g2 = (coef[i, at, :] for i in range(8))
            up = vx > 0.0
            x = {r: X[t, r, at, :] for r in used}
            if edge:
                x[0], x[1] = x[0] * low, x[1] * low
                x[10], x[11] = x[10] * high, x[11] * high
            for r in rows:
                f = x[r + 2]
                v = f * (diag - wall[r])
                v = v + a1 * jnp.where(up, x[r + 1], x[r + 3]) + a2 * jnp.where(up, x[r], x[r + 4])
                v = v + e1 * pltpu.roll(f, 1, 1) + e2 * pltpu.roll(f, 2, 1)
                v = v + g1 * pltpu.roll(f, NC - 1, 1) + g2 * pltpu.roll(f, NC - 2, 1)
                B[r, at, :] = v

        @pl.loop(0, MB // 64)
        def _(g):
            for i in range(8):
                modes(g * 8 + i)

    def ship(n, k, v):
        top = jnp.maximum(jnp.max(jnp.abs(v), axis=0, keepdims=True), 1e-20)
        power = jnp.ceil(jnp.log2(top))
        code = jnp.round(v * (jnp.exp2(-power) * TOP))
        Cs[n, k, 0:MB, :] = code.astype(jnp.int32).astype(jnp.int16)
        Cs[n, k, MB:MB + 16, :] = jnp.broadcast_to(power, (16, NC)).astype(jnp.int32).astype(jnp.int16)
        cc(n, k).start()

    def quarter(n, k):
        power = Cr[n, k, MB:MB + 16, :].astype(jnp.int32).astype(f32)[0:1, :]
        return Cr[n, k, 0:MB, :].astype(jnp.int32).astype(f32) * (jnp.exp2(power) * (0.25 / TOP))

    parts = (lambda at: (Wb[0, :, :, at],), lambda at: (Wb[1, :, :, at],))

    def times(w, at, g):
        total = None
        for part in parts[w](at):
            term = jnp.dot(part.reshape(MB, -1), g, preferred_element_type=f32)
            total = term if total is None else total + term
        return total

    def gain(w, *ns):
        if w == 0:
            for n in ns:
                for k in (0, 1):
                    cz_in(n, k, 1 - k).wait_recv()
                    cf_in(n, k).wait_recv()
        cells = [G[n].reshape(NMODES, NC) for n in ns]
        cells = cells[0] if len(ns) == 1 else jnp.concatenate(cells, axis=1)
        acc[:, 0:len(ns) * NC] = times(w, slice(None), cells)
        for i, n in enumerate(ns):
            ship(n, w, acc[:, i * NC:(i + 1) * NC])

    def layer(w, n, z_):
        at = [pl.ds(pl.multiple_of(hh * 4 * MB + z_ * MB, MB), MB) for hh in (0, 1)]
        cells = [G[n, z_], G[n, 4 + z_]]
        terms = list(zip(*(parts[w](a) for a in at)))
        left = [v.reshape(MB, MB) for term in terms for v in term]
        return jnp.dot(jnp.concatenate(left, axis=1), jnp.concatenate(cells * len(terms), axis=0),
                       preferred_element_type=f32)

    def early(n):
        cz_in(n, 0, 1).wait_recv()
        cz_in(n, 1, 0).wait_recv()
        for w in (0, 1):
            at = pl.ds(w * NC, NC)
            acc[:, at] = layer(w, n, z)

            @pl.loop(0, 2)
            def _(i):
                acc[:, at] += layer(w, n, (z + 1 + 2 * i) % 4)

    def late(n, w):
        if w == 0:
            cf_in(n, 0).wait_recv()
            cf_in(n, 1).wait_recv()
        ship(n, w, acc[:, w * NC:(w + 1) * NC] + layer(w, n, zz))

    def u1(j, k):
        cc(j, k).wait_recv()
        r = row(half_of[k], j)
        v = B[r] + quarter(j, k)
        X[1, 2 + r] = v
        Fs[1, r] = v.astype(bf16)
        cx(1, j, k).start()

    def u2(j):
        n = 4 + j
        cc(n, 0).wait_recv()
        cc(n, 1).wait_recv()
        at0 = half_of[0]
        D[pl.ds(3 - j, MB, stride=ROWS), :] = B[3 - j] + quarter(n, at0)
        D[pl.ds(4 + j, MB, stride=ROWS), :] = B[4 + j] + quarter(n, 1 - at0)

    share(1)
    share(2)
    first_send(0)
    cast_w(0)
    first_send(1)
    cast_w(1)
    share(0)
    share(3)
    w1(1)
    zown(0, 0)
    w1(2)
    first_send(2)
    zown(1, 0)
    coefs()
    first_send(3)
    cast_w(2)
    zown(0, 1)
    halo(0, 0)
    w2(1, 1)
    w2(2, 0)
    zown(1, 1)
    zfwd(0, 0)
    cast_w(3)
    w1(0)
    zfwd(1, 0)
    zfwd(0, 1)
    w1(3)
    zfwd(1, 1)
    w2(2, 1)
    w2(0, 1)
    w3(1)
    zown(2, 0)
    zown(3, 0)
    w2(0, 0)
    base(0, 0)
    w2(3, 0)
    w2(3, 1)
    gain(0, 0, 1)
    w3(0)
    zown(3, 1)
    w3(2)
    zfwd(2, 0)
    w2(1, 0)
    zown(2, 1)
    w3(3)
    wfin()
    gain(1, 0, 1)
    zfwd(3, 0)
    zfwd(3, 1)
    u1(0, 0)
    u1(1, 0)
    zfwd(2, 1)
    halo(0, 1)
    zown(4, 0)
    u1(0, 1)
    u1(1, 1)
    zown(5, 0)
    gain(0, 2, 3)
    zown(4, 1)
    gain(1, 2, 3)
    zown(5, 1)
    zfwd(5, 0)
    base(0, 1)
    zfwd(4, 1)
    zfwd(4, 0)
    u1(2, 0)
    zfwd(5, 1)
    u1(2, 1)
    u1(3, 0)
    zown(6, 0)
    zown(6, 1)
    u1(3, 1)
    halo(1, 1)
    zown(7, 0)
    gain(0, 4, 5)
    halo(1, 0)
    zfwd(6, 1)
    zfwd(6, 0)
    gain(1, 4, 5)
    zown(7, 1)
    zfwd(7, 0)
    base(1, 0)
    gain(0, 6)
    zfwd(7, 1)
    gain(1, 6)
    early(7)
    late(7, 0)
    late(7, 1)
    u2(1)
    base(1, 1)
    u2(0)
    u2(2)
    u2(3)
    store = pltpu.make_async_copy(D, out, lsem.at[0])
    store.start()

    for t in (0, 1):
        for k in (0, 1):
            ch(t, 0, k).wait_send()
            ch(t, 1, k).wait_send()
        for j in range(4):
            for k in (0, 1):
                cx(t, j, k).wait_send()
    for n in range(8):
        for k in (0, 1):
            cz(n, 0, k).wait_send()
            cz(n, 1, k).wait_send()
            cf(n, k).wait_send()
            cc(n, k).wait_send()
    for u in range(WU):
        cwx(u).wait_send()
        cwy(u, 0).wait_send()
        cwy(u, 1).wait_send()
        cwf(u).wait_send()
        for y_ in range(4):
            cwp(y_, u).wait_send()
    store.wait()


def body(distribution, courant, relax_rate, scatter_weight, cell_flags):
    vmem = pl.BlockSpec(memory_space=pltpu.VMEM)
    hbm = pl.BlockSpec(memory_space=pl.ANY)
    dma = pltpu.SemaphoreType.DMA
    out = pl.pallas_call(
        kernel,
        out_shape=jax.ShapeDtypeStruct((MB * ROWS, NC), f32),
        in_specs=[hbm, vmem, vmem, vmem, hbm],
        out_specs=hbm,
        scratch_shapes=[
            pltpu.VMEM((2, 12, MB, NC), f32),
            pltpu.VMEM((2, ROWS, MB, NC), bf16),
            pltpu.VMEM((8, 8, MB, NC), bf16),
            pltpu.VMEM((8, 2, MB + 16, NC), jnp.int16),
            pltpu.VMEM((8, 2, MB + 16, NC), jnp.int16),
            pltpu.VMEM((ROWS, MB, NC), f32),
            pltpu.VMEM((2, MB // WR, WR, NMODES), bf16),
            pltpu.VMEM((2, STAGE, NMODES), f32),
            pltpu.VMEM((64, NMODES), f32),
            pltpu.VMEM((WU, WR, NMODES), bf16),
            pltpu.VMEM((8, MB, NC), f32),
            pltpu.VMEM((MB, 2 * NC), f32),
            pltpu.VMEM((ROWS, 8, NC), f32),
            pltpu.VMEM((MB * ROWS, NC), f32),
            dma((4,)),
            dma((8, 2)), dma((8, 2)),
            dma((8, 2, 2)), dma((8, 2, 2)),
            dma((8, 2)), dma((8, 2)),
            dma((8, 2)), dma((8, 2)),
            dma((2, 2, 2)), dma((2, 2, 2)),
            dma((WU,)), dma((WU,)),
            dma((WU, 2)), dma((WU, 2)),
            dma((WU,)), dma((WU,)),
            dma((4, WU)), dma((4, WU)),
        ],
        compiler_params=pltpu.CompilerParams(
            collective_id=0, has_side_effects=True, vmem_limit_bytes=60 * 1024 * 1024),
    )(distribution.reshape(MB * ROWS, NC), courant, relax_rate.reshape(1, MB),
      cell_flags, scatter_weight)
    return out.reshape(distribution.shape)


def solution(mesh):
    in_specs = (
        P("mode", "tile", None),
        P(None, "mode"),
        P("mode"),
        P("mode", None),
        P("tile", None),
    )
    out_specs = P("mode", "tile", None)
    return jax.shard_map(body, mesh=mesh, in_specs=in_specs, out_specs=out_specs, check_vma=False)
```
